32 devices in a mesh: tm: 2 (over core), height: 8 (over z, y), head: 2 (over x).
Axes of the slice: x: 2, y: 2, z: 4, core: 2. Of those that a mesh axis runs over, the one named last changes fastest.
Arguments:
- queries: bfloat16 [4, 16, 64, 1280], P('tm', 'height', None, 'head'), may hold values from -22 to 22
- keys_values: bfloat16 [2, 4, 16, 64, 1280], P(None, 'tm', 'height', None, 'head'), may hold values from -7 to 7
- out_weight: bfloat16 [1280, 5120], P('head'), may hold values from -0.15625 to 0.15625
Outputs:
- mixed: bfloat16 [64, 4, 16, 5120], P('head', 'tm', 'height')
The draws below stay inside these ranges and needn't reach their ends.
All inputs are finite; a program needn't handle non-finite values.
Results may differ from the reference program's by a relative error of at most 0.013.
Values may be sent and summed in bfloat16 or wider, within the bound.
A program may use at most 128 MiB of HBM per device.

```python
import math
import jax
import jax.numpy as jnp
from jax import lax

D = 5120
HD = 128
HEAD_DEV = 5
COLS = 64
TILE = 16
WINDOW = 3
VALID_COLS = 52
HEADS = 10
FRAMES = 4
FRAME_ROWS = 16
VALID_ROWS = 14
N_HEAD = 2


def draw_queries(key, part):
    array_shape = (FRAMES, FRAME_ROWS, COLS, HEADS * HD)
    values = 2.5 * jax.random.truncated_normal(jax.random.fold_in(key, 1), -2.4, 2.4, array_shape, jnp.float32)
    return values.astype(jnp.bfloat16)


def draw_keys_values(key, part):
    array_shape = (2, FRAMES, FRAME_ROWS, COLS, HEADS * HD)
    values = jax.random.truncated_normal(jax.random.fold_in(key, 3), -6.0, 6.0, array_shape, jnp.float32)
    return values.astype(jnp.bfloat16)


def block_scale(own_key, shape, split, low, top_value):
    factor_of = 1.0
    for axis_at, parts in split:
        heights = jax.random.uniform(jax.random.fold_in(jax.random.fold_in(own_key, 6), axis_at), (parts,), jnp.float32, low / len(split), top_value / len(split))
        factor_of = factor_of * jnp.repeat(jnp.exp(heights), shape[axis_at] // parts).reshape((-1,) + (1,) * (len(shape) - 1 - axis_at))
    return factor_of


def bell_draw(stream_key, dims, deviation, reach, cuts=(), kind=jnp.bfloat16):
    drawn = deviation * jax.random.normal(stream_key, dims, jnp.float32)
    if cuts:
        drawn = drawn * block_scale(stream_key, dims, cuts, -0.22, 0.18)
    return jnp.clip(drawn, -reach, reach).astype(kind)


def setup_inputs(seed: int = 0) -> dict:
    keys = jax.random.split(jax.random.key(seed), 4)
    queries = draw_queries(jax.random.fold_in(keys[3], 71), 0)
    keys_values = draw_keys_values(jax.random.fold_in(keys[3], 71), 0)
    out_weight = bell_draw(keys[2], (HEADS * HD, D), (HEADS * HD) ** -0.5, 0.15625, ((0, 2),))
    return dict(queries=queries, keys_values=keys_values, out_weight=out_weight)


masked_value = -1e+30

def reference(queries, keys_values, out_weight):
    row_tiles = FRAME_ROWS // TILE
    col_tiles = COLS // TILE
    frame_span = min(FRAMES, WINDOW)
    row_span = min(row_tiles, WINDOW)
    col_span = min(col_tiles, WINDOW)
    width_all = HEADS * HD
    score_scale = 1.0 / math.sqrt(HD)
    block_count = FRAMES * row_tiles * col_tiles

    def one_block(block_id):
        frame_id = block_id // (row_tiles * col_tiles)
        row_tile = block_id // col_tiles % row_tiles
        col_tile = block_id % col_tiles
        frame_low = jnp.clip(frame_id - 1, 0, FRAMES - frame_span).astype(jnp.int32)
        row_low = (jnp.clip(row_tile - 1, 0, row_tiles - row_span) * TILE).astype(jnp.int32)
        col_low = (jnp.clip(col_tile - 1, 0, col_tiles - col_span) * TILE).astype(jnp.int32)
        zero_index = jnp.zeros((), jnp.int32)
        query_block = lax.dynamic_slice(queries, (frame_id.astype(jnp.int32), (row_tile * TILE).astype(jnp.int32), (col_tile * TILE).astype(jnp.int32), zero_index), (1, TILE, TILE, width_all))
        key_block = lax.dynamic_slice(keys_values, (zero_index, frame_low, row_low, col_low, zero_index), (2, frame_span, row_span * TILE, col_span * TILE, width_all))
        key_rows = row_low + jnp.arange(row_span * TILE, dtype=jnp.int32)
        key_cols = col_low + jnp.arange(col_span * TILE, dtype=jnp.int32)
        content = (key_rows[:, None] < VALID_ROWS) & (key_cols[None, :] < VALID_COLS)
        content = jnp.broadcast_to(content[None], (frame_span, row_span * TILE, col_span * TILE)).reshape(-1)
        query_vec = query_block.reshape(TILE * TILE, HEADS, HD).astype(jnp.float32)
        key_vec = key_block[0].reshape(-1, HEADS, HD).astype(jnp.float32)
        value_vec = key_block[1].reshape(-1, HEADS, HD).astype(jnp.float32)
        scores = jnp.einsum('qhd,khd->hqk', query_vec, key_vec) * score_scale
        scores = jnp.where(content[None, None, :], scores, masked_value)
        largest = lax.optimization_barrier(jnp.max(scores, axis=2, keepdims=True))
        weights = jnp.where(content[None, None, :], jnp.exp(scores - largest), 0.0)
        total = lax.optimization_barrier(jnp.sum(weights, axis=2))
        rounded = lax.optimization_barrier(weights.astype(jnp.bfloat16)).astype(jnp.float32)
        attended = jnp.einsum('hqk,khd->qhd', rounded, value_vec) / jnp.transpose(total)[:, :, None]
        return attended.reshape(TILE, TILE, width_all).astype(jnp.bfloat16)
    blocks = lax.map(one_block, jnp.arange(block_count, dtype=jnp.int32))
    attended = blocks.reshape(FRAMES, row_tiles, col_tiles, TILE, TILE, width_all)
    attended = attended.transpose(0, 1, 3, 2, 4, 5).reshape(FRAMES * FRAME_ROWS * COLS, width_all)
    group_width = HEAD_DEV * HD
    summed = jnp.zeros((FRAMES * FRAME_ROWS * COLS, D), jnp.float32)
    for group_id in range(N_HEAD):
        lower = group_id * group_width
        partial_sum = jnp.dot(attended[:, lower:lower + group_width], out_weight[lower:lower + group_width], preferred_element_type=jnp.float32)
        summed = summed + lax.optimization_barrier(partial_sum.astype(jnp.bfloat16)).astype(jnp.float32)
    mixed = summed.astype(jnp.bfloat16).reshape(FRAMES, FRAME_ROWS, COLS, D)
    return jnp.transpose(mixed, (2, 0, 1, 3))
```

```python
import functools
import math

import jax
import jax.numpy as jnp
from jax import lax
from jax.experimental import pallas as pl
from jax.experimental.pallas import tpu as pltpu
from jax.sharding import PartitionSpec as P

HD = 128
TILE = 16
WINDOW = 3
PAD_ROWS = 2
VALID_COLS = 52
MESH = pl.DeviceIdType.MESH
UP, DOWN, ACROSS, CORE = 0, 1, 2, 3
PIECE = 512

masked_value = -1e30


def kernel(
    n_height,
    n_head,
    rows_dev,
    q_ref,
    kv_hbm,
    w_hbm,
    out_ref,
    kv,
    w,
    bias,
    top,
    total,
    acc,
    att,
    outbox,
    inbox,
    own_sem,
    w_sem,
    send_sem,
    recv_sem,
    part_send,
    part_recv,
):
    lines = n_height // 2
    tokens, width = q_ref.shape
    heads = width // HD
    key_count = rows_dev * VALID_COLS
    model = w.shape[1]
    pieces = model // PIECE
    share = tokens // n_head
    last = lines - 1

    side = lax.axis_index("tm")
    place = lax.axis_index("height")
    group = lax.axis_index("head")
    z = place // 2
    y = place % 2
    has_own = place < n_height - 1

    weight_copy = pltpu.make_async_copy(w_hbm, w, w_sem)
    weight_copy.start()
    own_copy = pltpu.make_async_copy(kv_hbm, kv.at[place, 0:2], own_sem)
    own_copy.start()

    barrier = pltpu.get_barrier_semaphore()

    def greet(target):
        pl.semaphore_signal(barrier, inc=1, device_id=target, device_id_type=MESH)

    @pl.when(z < last)
    def _():
        greet({"height": place + 2})

    @pl.when(z > 0)
    def _():
        greet({"height": place - 2})

    greet({"height": place + 1 - 2 * y})
    greet({"tm": 1 - side})
    for step in range(1, n_head):
        greet({"head": lax.rem(group + step, n_head)})

    def link(direction, slot, frame):
        target = {
            UP: {"height": jnp.minimum(place + 2, n_height - 1)},
            DOWN: {"height": jnp.maximum(place - 2, 0)},
            ACROSS: {"height": place + 1 - 2 * y},
            CORE: {"tm": 1 - side},
        }[direction]
        landing = 2 if direction == CORE else frame
        return pltpu.make_async_remote_copy(
            src_ref=kv.at[slot, frame],
            dst_ref=kv.at[slot, landing],
            send_sem=send_sem.at[direction, slot, frame],
            recv_sem=recv_sem.at[slot, landing],
            device_id=target,
            device_id_type=MESH,
        )

    def on_line(d, sign):
        zs = z + sign * d
        real = (zs >= 0) & (zs < lines) & ((d > 0) | has_own)
        if sign > 0:
            real = real & (d > 0)
        proxied = (zs == last) & (y == 1)
        slot = jnp.clip(jnp.where(proxied, 2 * last, 2 * zs + y), 0, n_height - 1)
        up = real & (z < last) & ((sign < 0) | (d == 0))
        down = real & (z > 0) & ((sign > 0) | (d == 0))
        across = real & ((zs != last) | ((z == last) & (y == 0)))
        return real, slot, up, down, across

    def off_line(d, sign):
        zs = z + sign * d
        proxy = (z == last) & (y == 1) & (zs == last)
        real = (d >= 0) & (zs >= 0) & (zs < lines) & ((zs != last) | proxy)
        if sign > 0:
            real = real & (d > 0)
        slot = jnp.clip(2 * zs + 1 - y, 0, n_height - 1)
        return real, slot, proxy & real

    def line_sends(d, sign, act):
        real, slot, up, down, across = on_line(d, sign)
        for frame in (0, 1):
            if act == "start":

                @pl.when(real & (d > 0))
                def _():
                    link(UP, slot, frame).wait_recv()

            for flag, direction in ((up, UP), (down, DOWN), (across, ACROSS)):

                @pl.when(flag)
                def _():
                    copy = link(direction, slot, frame)
                    copy.start() if act == "start" else copy.wait_send()

            if frame == 0:

                @pl.when(real)
                def _():
                    copy = link(CORE, slot, 0)
                    copy.start() if act == "start" else copy.wait_send()

    def cross_sends(d, sign, act):
        real, slot, proxy = off_line(d, sign)
        for frame in (0, 1):
            if act == "start":

                @pl.when(real)
                def _():
                    link(ACROSS, slot, frame).wait_recv()

            @pl.when(proxy)
            def _():
                copy = link(DOWN, slot, frame)
                copy.start() if act == "start" else copy.wait_send()

            if frame == 0:

                @pl.when(real)
                def _():
                    copy = link(CORE, slot, 0)
                    copy.start() if act == "start" else copy.wait_send()

    factor = math.log2(math.e) / math.sqrt(HD)

    def attend(slot):
        pltpu.make_async_remote_copy(
            src_ref=kv.at[slot, 2],
            dst_ref=kv.at[slot, 2],
            send_sem=send_sem.at[CORE, slot, 0],
            recv_sem=recv_sem.at[slot, 2],
            device_id={"tm": 1 - side},
            device_id_type=MESH,
        ).wait_recv()
        for head in range(heads):
            lanes = slice(head * HD, (head + 1) * HD)
            query = q_ref[:, lanes]
            scores = []
            for frame in range(3):
                key = kv[slot, frame, 0:key_count, lanes]
                score = lax.dot_general(
                    query, key, (((1,), (1,)), ((), ())), preferred_element_type=jnp.float32
                )
                scores.append(score * factor + bias[...])
            largest = jnp.maximum(jnp.maximum(scores[0], scores[1]), scores[2])
            old_top = top[head]
            new_top = jnp.maximum(old_top, jnp.max(largest, axis=1, keepdims=True))
            alpha = jnp.exp2(old_top - new_top)
            top[head] = new_top
            added = None
            mixed = None
            for frame in range(3):
                weight = jnp.exp2(scores[frame] - new_top)
                value = kv[slot, frame, key_count : 2 * key_count, lanes]
                part = jnp.dot(
                    weight.astype(jnp.bfloat16), value, preferred_element_type=jnp.float32
                )
                added = weight if added is None else added + weight
                mixed = part if mixed is None else mixed + part
            total[head] = total[head] * alpha + added
            acc[head] = acc[head] * alpha + mixed

    own_copy.wait()
    arrivals = (
        2 + (n_head - 1) + jnp.where(z < last, 1, 0) + jnp.where(z > 0, 1, 0)
    ).astype(jnp.int32)
    pl.semaphore_wait(barrier, arrivals)
    line_sends(0, -1, "start")

    lane = lax.broadcasted_iota(jnp.int32, (tokens, key_count), 1)
    column = lax.rem(lane, VALID_COLS)
    right_half = lax.broadcasted_iota(jnp.int32, (tokens, key_count), 0) >= tokens // 2
    seen = jnp.where(right_half, column - TILE, (WINDOW * TILE - 1) - column) >= 0
    bias[...] = jnp.where(seen, 0.0, masked_value)
    top[...] = jnp.full_like(top, masked_value)
    total[...] = jnp.zeros_like(total)
    acc[...] = jnp.zeros_like(acc)

    def round_body(d, carry):
        def one(j, inner):
            real = None
            sign_up = lax.rem(j, 2)
            line_m, line_p = on_line(d - 1, -1), on_line(d - 1, 1)
            off_m, off_p = off_line(d - 2, -1), off_line(d - 2, 1)
            first = j < 2
            real = jnp.where(
                first,
                jnp.where(sign_up == 0, line_m[0].astype(jnp.int32), line_p[0].astype(jnp.int32)),
                jnp.where(sign_up == 0, off_m[0].astype(jnp.int32), off_p[0].astype(jnp.int32)),
            )
            slot = jnp.where(
                first,
                jnp.where(sign_up == 0, line_m[1], line_p[1]),
                jnp.where(sign_up == 0, off_m[1], off_p[1]),
            )

            @pl.when(real == 1)
            def _():
                attend(slot)

            return inner

        lax.fori_loop(0, 4, one, 0)
        line_sends(d, -1, "start")
        line_sends(d, 1, "start")
        cross_sends(d - 1, -1, "start")
        cross_sends(d - 1, 1, "start")
        return carry

    lax.fori_loop(1, lines + 2, round_body, 0)

    for head in range(heads):
        whole = jnp.sum(total[head], axis=1, keepdims=True)
        att[:, head * HD : (head + 1) * HD] = (acc[head] / whole).astype(jnp.bfloat16)
    weight_copy.wait()

    def product(first_row, at):
        return jnp.dot(
            att[pl.ds(pl.multiple_of(first_row, share), share), :],
            w[:, pl.ds(pl.multiple_of(at * PIECE, PIECE), PIECE)],
            preferred_element_type=jnp.float32,
        ).astype(jnp.bfloat16)

    def parcel(step, at):
        return pltpu.make_async_remote_copy(
            src_ref=outbox.at[step - 1, at],
            dst_ref=inbox.at[step - 1, at],
            send_sem=part_send.at[step - 1, at],
            recv_sem=part_recv.at[step - 1, at],
            device_id={"head": lax.rem(group + step, n_head)},
            device_id_type=MESH,
        )

    for step in range(1, n_head):

        def ship(at, carry):
            outbox[step - 1, at] = product(lax.rem(group + step, n_head) * share, at)
            parcel(step, at).start()
            return carry

        lax.fori_loop(0, pieces, ship, 0)

    def collect(at, carry):
        summed = product(group * share, at).astype(jnp.float32)
        for step in range(1, n_head):
            parcel(step, at).wait_recv()
            summed = summed + inbox[step - 1, at].astype(jnp.float32)
        out_ref[:, pl.ds(pl.multiple_of(at * PIECE, PIECE), PIECE)] = summed.astype(jnp.bfloat16)
        return carry

    lax.fori_loop(0, pieces, collect, 0)

    for step in range(1, n_head):

        def settle(at, carry):
            parcel(step, at).wait_send()
            return carry

        lax.fori_loop(0, pieces, settle, 0)

    def drain(d, carry):
        line_sends(d, -1, "wait")
        line_sends(d, 1, "wait")
        cross_sends(d, -1, "wait")
        cross_sends(d, 1, "wait")
        return carry

    lax.fori_loop(0, lines, drain, 0)


def on_device(n_height, n_head, queries, keys_values, out_weight):
    frames_dev, rows_dev, col_count, width = queries.shape
    model = out_weight.shape[1]
    heads = width // HD
    tokens = frames_dev * rows_dev * col_count
    key_count = rows_dev * VALID_COLS
    share = tokens // n_head
    pieces = model // PIECE
    assert frames_dev == 2 and rows_dev == PAD_ROWS and col_count == 4 * TILE
    assert n_height % 2 == 0 and n_height * rows_dev <= WINDOW * TILE
    side = lax.axis_index("tm")
    ordered = jnp.transpose(queries, (2, 0, 1, 3)).reshape(tokens, width)
    packed = jnp.transpose(keys_values[:, :, :, :VALID_COLS], (1, 0, 2, 3, 4))
    packed = packed.reshape(frames_dev, 2 * key_count, width)
    packed = jnp.where(side == 0, packed[::-1], packed)
    others = n_head - 1
    out = pl.pallas_call(
        functools.partial(kernel, n_height, n_head, rows_dev),
        out_shape=jax.ShapeDtypeStruct((share, model), jnp.bfloat16),
        in_specs=[
            pl.BlockSpec(memory_space=pltpu.VMEM),
            pl.BlockSpec(memory_space=pl.ANY),
            pl.BlockSpec(memory_space=pl.ANY),
        ],
        out_specs=pl.BlockSpec(memory_space=pltpu.VMEM),
        scratch_shapes=[
            pltpu.VMEM((n_height, 3, 2 * key_count, width), jnp.bfloat16),
            pltpu.VMEM((width, model), jnp.bfloat16),
            pltpu.VMEM((tokens, key_count), jnp.float32),
            pltpu.VMEM((heads, tokens, 1), jnp.float32),
            pltpu.VMEM((heads, tokens, key_count), jnp.float32),
            pltpu.VMEM((heads, tokens, HD), jnp.float32),
            pltpu.VMEM((tokens, width), jnp.bfloat16),
            pltpu.VMEM((others, pieces, share, PIECE), jnp.bfloat16),
            pltpu.VMEM((others, pieces, share, PIECE), jnp.bfloat16),
            pltpu.SemaphoreType.DMA,
            pltpu.SemaphoreType.DMA,
            pltpu.SemaphoreType.DMA((4, n_height, 2)),
            pltpu.SemaphoreType.DMA((n_height, 3)),
            pltpu.SemaphoreType.DMA((others, pieces)),
            pltpu.SemaphoreType.DMA((others, pieces)),
        ],
        compiler_params=pltpu.CompilerParams(
            collective_id=0, has_side_effects=True, vmem_limit_bytes=56 * 2**20
        ),
        name="tile_attention",
    )(ordered, packed, out_weight)
    return out.reshape(col_count // n_head, frames_dev, rows_dev, model)


def solution(mesh):
    placed = (
        P("tm", "height", None, "head"),
        P(None, "tm", "height", None, "head"),
        P("head", None),
    )
    return jax.shard_map(
        functools.partial(on_device, mesh.shape["height"], mesh.shape["head"]),
        mesh=mesh,
        in_specs=placed,
        out_specs=P("head", "tm", "height", None),
        check_vma=False,
    )
```

```python
import functools
import math

import jax
import jax.numpy as jnp
from jax import lax
from jax.experimental import pallas as pl
from jax.experimental.pallas import tpu as pltpu
from jax.sharding import PartitionSpec as P

HD = 128
TILE = 16
WINDOW = 3
PAD_ROWS = 2
VALID_COLS = 52
MESH = pl.DeviceIdType.MESH
UP, DOWN, ACROSS, CORE = 0, 1, 2, 3
PIECE = 512
ROW_CUTS = (0, 208)
CUTS = len(ROW_CUTS) - 1
SHARED_PIECES = 6
SHARED_CUTS = 4

masked_value = -1e30


def kernel(
    n_height,
    n_head,
    rows_dev,
    q_ref,
    kv_hbm,
    w_hbm,
    out_ref,
    kv,
    w,
    bias,
    top,
    total,
    acc,
    att,
    outbox,
    inbox,
    own_sem,
    w_sem,
    send_sem,
    recv_sem,
    part_send,
    part_recv,
    w_far,
    att_far,
    far_send,
    pass_send,
    far_recv,
    att_sems,
):
    lines = n_height // 2
    tokens, width = q_ref.shape
    heads = width // HD
    key_count = rows_dev * VALID_COLS
    model = w.shape[1]
    shared = shared_width(n_head)
    far_width = shared // SHARED_CUTS
    pieces = (model - shared) // PIECE
    share = tokens // n_head
    last = lines - 1

    side = lax.axis_index("tm")
    place = lax.axis_index("height")
    group = lax.axis_index("head")
    z = place // 2
    y = place % 2
    has_own = place < n_height - 1

    weight_copy = pltpu.make_async_copy(w_hbm, w, w_sem)
    weight_copy.start()
    own_copy = pltpu.make_async_copy(kv_hbm, kv.at[place, 0:2], own_sem)
    own_copy.start()

    barrier = pltpu.get_barrier_semaphore()

    def greet(target):
        pl.semaphore_signal(barrier, inc=1, device_id=target, device_id_type=MESH)

    @pl.when(z < last)
    def _():
        greet({"height": place + 2})

    @pl.when(z > 0)
    def _():
        greet({"height": place - 2})

    greet({"height": place + 1 - 2 * y})
    greet({"tm": 1 - side})
    for step in range(1, n_head):
        greet({"head": lax.rem(group + step, n_head)})

    def link(direction, slot, frame, cut):
        target = {
            UP: {"height": jnp.minimum(place + 2, n_height - 1)},
            DOWN: {"height": jnp.maximum(place - 2, 0)},
            ACROSS: {"height": place + 1 - 2 * y},
            CORE: {"tm": 1 - side},
        }[direction]
        landing = 2 if direction == CORE else frame
        span = pl.ds(ROW_CUTS[cut], ROW_CUTS[cut + 1] - ROW_CUTS[cut])
        return pltpu.make_async_remote_copy(
            src_ref=kv.at[slot, frame, span],
            dst_ref=kv.at[slot, landing, span],
            send_sem=send_sem.at[direction, slot, frame * CUTS + cut],
            recv_sem=recv_sem.at[slot, landing * CUTS + cut],
            device_id=target,
            device_id_type=MESH,
        )

    def on_line(d, sign):
        zs = z + sign * d
        real = (zs >= 0) & (zs < lines) & ((d > 0) | has_own)
        if sign > 0:
            real = real & (d > 0)
        proxied = (zs == last) & (y == 1)
        slot = jnp.clip(jnp.where(proxied, 2 * last, 2 * zs + y), 0, n_height - 1)
        up = real & (z < last) & ((sign < 0) | (d == 0))
        down = real & (z > 0) & ((sign > 0) | (d == 0))
        across = real & ((zs != last) | ((z == last) & (y == 0)))
        return real, slot, up, down, across

    def off_line(d, sign):
        zs = z + sign * d
        proxy = (z == last) & (y == 1) & (zs == last)
        real = (d >= 0) & (zs >= 0) & (zs < lines) & ((zs != last) | proxy)
        if sign > 0:
            real = real & (d > 0)
        slot = jnp.clip(2 * zs + 1 - y, 0, n_height - 1)
        return real, slot, proxy & real

    def act_on(flag, copy, act):
        @pl.when(flag)
        def _():
            getattr(copy, act)()

    def line_sends(d, act):
        sides = [on_line(d, -1), on_line(d, 1)]
        _, proxy_slot, proxy = off_line(0, -1)
        for frame in (0, 1):
            for cut in range(CUTS):
                for real, slot, up, down, across in sides:
                    if act == "start":
                        act_on(real & (d > 0), link(UP, slot, frame, cut), "wait_recv")
                    act_on(up, link(UP, slot, frame, cut), act)
                    act_on(down, link(DOWN, slot, frame, cut), act)
                    act_on(across, link(ACROSS, slot, frame, cut), act)
                    if frame == 0:
                        act_on(real, link(CORE, slot, 0, cut), act)
                now = proxy & (d == 1)
                if act == "start":
                    act_on(now, link(ACROSS, proxy_slot, frame, cut), "wait_recv")
                act_on(now, link(DOWN, proxy_slot, frame, cut), act)
                if frame == 0:
                    act_on(now, link(CORE, proxy_slot, 0, cut), act)

    def cross_sends(d, act):
        sides = [off_line(d, -1), off_line(d, 1)]
        for frame in (0, 1):
            for cut in range(CUTS):
                for real, slot, proxy in sides:
                    plain = real & jnp.logical_not(proxy)
                    if act == "start":
                        act_on(plain, link(ACROSS, slot, frame, cut), "wait_recv")
                    if frame == 0:
                        act_on(plain, link(CORE, slot, 0, cut), act)

    def far_weight(step):
        at = 2 * side + step
        first = pl.multiple_of(model - shared + at * far_width, HD)
        return pltpu.make_async_remote_copy(
            src_ref=w_hbm.at[:, pl.ds(first, far_width)],
            dst_ref=w_far.at[at],
            send_sem=far_send.at[step],
            recv_sem=far_recv.at[at],
            device_id={"head": 1 - group},
            device_id_type=MESH,
        )

    def pass_weight(step, owner):
        at = 2 * owner + step
        return pltpu.make_async_remote_copy(
            src_ref=w_far.at[at],
            dst_ref=w_far.at[at],
            send_sem=pass_send.at[step],
            recv_sem=far_recv.at[at],
            device_id={"tm": 1 - side},
            device_id_type=MESH,
        )

    def relay_weight(step):
        far_weight(step).wait_recv()
        pass_weight(step, side).start()

    factor = math.log2(math.e) / math.sqrt(HD)

    def attend(slot):
        for cut in range(CUTS):
            link(CORE, slot, 0, cut).wait_recv()
        for head in range(heads):
            lanes = slice(head * HD, (head + 1) * HD)
            query = q_ref[:, lanes]
            scores = []
            for frame in range(3):
                key = kv[slot, frame, 0:key_count, lanes]
                score = lax.dot_general(
                    query, key, (((1,), (1,)), ((), ())), preferred_element_type=jnp.float32
                )
                scores.append(score * factor + bias[...])
            largest = jnp.maximum(jnp.maximum(scores[0], scores[1]), scores[2])
            old_top = top[head]
            new_top = jnp.maximum(old_top, jnp.max(largest, axis=1, keepdims=True))
            alpha = jnp.exp2(old_top - new_top)
            top[head] = new_top
            added = None
            mixed = None
            for frame in range(3):
                weight = jnp.exp2(scores[frame] - new_top)
                value = kv[slot, frame, key_count : 2 * key_count, lanes]
                part = jnp.dot(
                    weight.astype(jnp.bfloat16), value, preferred_element_type=jnp.float32
                )
                added = weight if added is None else added + weight
                mixed = part if mixed is None else mixed + part
            total[head] = total[head] * alpha + added
            acc[head] = acc[head] * alpha + mixed

    own_copy.wait()
    arrivals = (
        2 + (n_head - 1) + jnp.where(z < last, 1, 0) + jnp.where(z > 0, 1, 0)
    ).astype(jnp.int32)
    pl.semaphore_wait(barrier, arrivals)
    line_sends(0, "start")
    if shared:
        far_weight(0).start()
        far_weight(1).start()

    lane = lax.broadcasted_iota(jnp.int32, (tokens, key_count), 1)
    column = lax.rem(lane, VALID_COLS)
    right_half = lax.broadcasted_iota(jnp.int32, (tokens, key_count), 0) >= tokens // 2
    seen = jnp.where(right_half, column - TILE, (WINDOW * TILE - 1) - column) >= 0
    bias[...] = jnp.where(seen, 0.0, masked_value)
    top[...] = jnp.full_like(top, masked_value)
    total[...] = jnp.zeros_like(total)
    acc[...] = jnp.zeros_like(acc)

    def round_body(d, carry):
        if shared:

            @pl.when(d == 3)
            def _():
                relay_weight(0)

            @pl.when(d == lines + 1)
            def _():
                relay_weight(1)

        def one(j, inner):
            real = None
            sign_up = lax.rem(j, 2)
            line_m, line_p = on_line(d - 1, -1), on_line(d - 1, 1)
            off_m, off_p = off_line(d - 2, -1), off_line(d - 2, 1)
            first = j < 2
            real = jnp.where(
                first,
                jnp.where(sign_up == 0, line_m[0].astype(jnp.int32), line_p[0].astype(jnp.int32)),
                jnp.where(sign_up == 0, off_m[0].astype(jnp.int32), off_p[0].astype(jnp.int32)),
            )
            slot = jnp.where(
                first,
                jnp.where(sign_up == 0, line_m[1], line_p[1]),
                jnp.where(sign_up == 0, off_m[1], off_p[1]),
            )

            @pl.when(real == 1)
            def _():
                attend(slot)

            return inner

        lax.fori_loop(0, 4, one, 0)
        line_sends(d, "start")
        cross_sends(d - 1, "start")
        return carry

    lax.fori_loop(1, lines + 2, round_body, 0)

    for head in range(heads):
        whole = jnp.sum(total[head], axis=1, keepdims=True)
        att[:, head * HD : (head + 1) * HD] = (acc[head] / whole).astype(jnp.bfloat16)
    weight_copy.wait()

    def product(first_row, at):
        return jnp.dot(
            att[pl.ds(pl.multiple_of(first_row, share), share), :],
            w[:, pl.ds(pl.multiple_of(at * PIECE, PIECE), PIECE)],
            preferred_element_type=jnp.float32,
        ).astype(jnp.bfloat16)

    def parcel(step, at):
        return pltpu.make_async_remote_copy(
            src_ref=outbox.at[step - 1, at],
            dst_ref=inbox.at[step - 1, at],
            send_sem=part_send.at[step - 1, at],
            recv_sem=part_recv.at[step - 1, at],
            device_id={"head": lax.rem(group + step, n_head)},
            device_id_type=MESH,
        )

    if shared:
        far_rows = pl.ds(pl.multiple_of((1 - group) * share, share), share)
        att_copy = pltpu.make_async_remote_copy(
            src_ref=att.at[far_rows],
            dst_ref=att_far,
            send_sem=att_sems.at[0],
            recv_sem=att_sems.at[1],
            device_id={"head": 1 - group},
            device_id_type=MESH,
        )
        att_copy.start()

    for step in range(1, n_head):

        def ship(at, carry):
            outbox[step - 1, at] = product(lax.rem(group + step, n_head) * share, at)
            parcel(step, at).start()
            return carry

        lax.fori_loop(0, pieces, ship, 0)

    if shared:
        own_rows = pl.ds(pl.multiple_of(group * share, share), share)
        pass_weight(0, 1 - side).wait_recv()
        pass_weight(1, 1 - side).wait_recv()
        att_copy.wait_recv()
        for at in range(SHARED_CUTS):
            first = model - shared + at * far_width
            span = slice(first, first + far_width)
            near = jnp.dot(att[own_rows, :], w[:, span], preferred_element_type=jnp.float32)
            far = jnp.dot(att_far[...], w_far[at], preferred_element_type=jnp.float32)
            near = near.astype(jnp.bfloat16).astype(jnp.float32)
            far = far.astype(jnp.bfloat16).astype(jnp.float32)
            out_ref[:, span] = (near + far).astype(jnp.bfloat16)

    def collect(at, carry):
        summed = product(group * share, at).astype(jnp.float32)
        for step in range(1, n_head):
            parcel(step, at).wait_recv()
            summed = summed + inbox[step - 1, at].astype(jnp.float32)
        out_ref[:, pl.ds(pl.multiple_of(at * PIECE, PIECE), PIECE)] = summed.astype(jnp.bfloat16)
        return carry

    lax.fori_loop(0, pieces, collect, 0)

    for step in range(1, n_head):

        def settle(at, carry):
            parcel(step, at).wait_send()
            return carry

        lax.fori_loop(0, pieces, settle, 0)

    if shared:
        att_copy.wait_send()
        for step in range(2):
            far_weight(step).wait_send()
            pass_weight(step, side).wait_send()

    def drain(d, carry):
        line_sends(d, "wait_send")
        cross_sends(d, "wait_send")
        return carry

    lax.fori_loop(0, lines, drain, 0)


def shared_width(n_head):
    return SHARED_PIECES * PIECE if n_head == 2 else 0


def on_device(n_height, n_head, queries, keys_values, out_weight):
    frames_dev, rows_dev, col_count, width = queries.shape
    model = out_weight.shape[1]
    heads = width // HD
    tokens = frames_dev * rows_dev * col_count
    key_count = rows_dev * VALID_COLS
    share = tokens // n_head
    shared = shared_width(n_head)
    far_width = shared // SHARED_CUTS
    pieces = (model - shared) // PIECE
    assert frames_dev == 2 and rows_dev == PAD_ROWS and col_count == 4 * TILE
    assert n_height % 2 == 0 and n_height * rows_dev <= WINDOW * TILE
    side = lax.axis_index("tm")
    ordered = jnp.transpose(queries, (2, 0, 1, 3)).reshape(tokens, width)
    packed = jnp.transpose(keys_values[:, :, :, :VALID_COLS], (1, 0, 2, 3, 4))
    packed = packed.reshape(frames_dev, 2 * key_count, width)
    packed = jnp.where(side == 0, packed[::-1], packed)
    others = n_head - 1
    out = pl.pallas_call(
        functools.partial(kernel, n_height, n_head, rows_dev),
        out_shape=jax.ShapeDtypeStruct((share, model), jnp.bfloat16),
        in_specs=[
            pl.BlockSpec(memory_space=pltpu.VMEM),
            pl.BlockSpec(memory_space=pl.ANY),
            pl.BlockSpec(memory_space=pl.ANY),
        ],
        out_specs=pl.BlockSpec(memory_space=pltpu.VMEM),
        scratch_shapes=[
            pltpu.VMEM((n_height, 3, 2 * key_count, width), jnp.bfloat16),
            pltpu.VMEM((width, model), jnp.bfloat16),
            pltpu.VMEM((tokens, key_count), jnp.float32),
            pltpu.VMEM((heads, tokens, 1), jnp.float32),
            pltpu.VMEM((heads, tokens, key_count), jnp.float32),
            pltpu.VMEM((heads, tokens, HD), jnp.float32),
            pltpu.VMEM((tokens, width), jnp.bfloat16),
            pltpu.VMEM((others, pieces, share, PIECE), jnp.bfloat16),
            pltpu.VMEM((others, pieces, share, PIECE), jnp.bfloat16),
            pltpu.SemaphoreType.DMA,
            pltpu.SemaphoreType.DMA,
            pltpu.SemaphoreType.DMA((4, n_height, 2 * CUTS)),
            pltpu.SemaphoreType.DMA((n_height, 3 * CUTS)),
            pltpu.SemaphoreType.DMA((others, pieces)),
            pltpu.SemaphoreType.DMA((others, pieces)),
            pltpu.VMEM((SHARED_CUTS, width, max(far_width, HD)), jnp.bfloat16),
            pltpu.VMEM((share, width), jnp.bfloat16),
            pltpu.SemaphoreType.DMA((2,)),
            pltpu.SemaphoreType.DMA((2,)),
            pltpu.SemaphoreType.DMA((SHARED_CUTS,)),
            pltpu.SemaphoreType.DMA((2,)),
        ],
        compiler_params=pltpu.CompilerParams(
            collective_id=0, has_side_effects=True, vmem_limit_bytes=56 * 2**20
        ),
        name="tile_attention",
    )(ordered, packed, out_weight)
    return out.reshape(col_count // n_head, frames_dev, rows_dev, model)


def solution(mesh):
    placed = (
        P("tm", "height", None, "head"),
        P(None, "tm", "height", None, "head"),
        P("head", None),
    )
    return jax.shard_map(
        functools.partial(on_device, mesh.shape["height"], mesh.shape["head"]),
        mesh=mesh,
        in_specs=placed,
        out_specs=P("head", "tm", "height", None),
        check_vma=False,
    )
```

```python
import functools
import math

import jax
import jax.numpy as jnp
from jax import lax
from jax.experimental import pallas as pl
from jax.experimental.pallas import tpu as pltpu
from jax.sharding import PartitionSpec as P

HD = 128
TILE = 16
WINDOW = 3
PAD_ROWS = 2
VALID_COLS = 52
MESH = pl.DeviceIdType.MESH
UP, DOWN, ACROSS, CORE = 0, 1, 2, 3
PIECE = 512
ROW_CUTS = (0, 208)
CUTS = len(ROW_CUTS) - 1
SHARED_PIECES = 6
SHARED_CUTS = 4
COPY_CUTS = 4

masked_value = -1e30


def kernel(
    n_height,
    n_head,
    rows_dev,
    raw_ref,
    kv_hbm,
    w_hbm,
    out_ref,
    kv,
    w,
    bias,
    top,
    total,
    acc,
    att,
    outbox,
    inbox,
    own_sem,
    w_sem,
    send_sem,
    recv_sem,
    part_send,
    part_recv,
    w_far,
    att_far,
    far_send,
    pass_send,
    far_recv,
    att_sems,
    q_ref,
    own_raw,
):
    lines = n_height // 2
    tokens, width = raw_ref.shape
    heads = width // HD
    key_count = rows_dev * VALID_COLS
    model = w.shape[1]
    shared = shared_width(n_head)
    far_width = shared // SHARED_CUTS
    pieces = (model - shared) // PIECE
    share = tokens // n_head
    last = lines - 1

    side = lax.axis_index("tm")
    place = lax.axis_index("height")
    group = lax.axis_index("head")
    z = place // 2
    y = place % 2
    has_own = place < n_height - 1

    weight_copy = pltpu.make_async_copy(w_hbm, w, w_sem)
    weight_copy.start()
    own_copy = pltpu.make_async_copy(kv_hbm, own_raw, own_sem)
    own_copy.start()

    barrier = pltpu.get_barrier_semaphore()

    def greet(target):
        pl.semaphore_signal(barrier, inc=1, device_id=target, device_id_type=MESH)

    @pl.when(z < last)
    def _():
        greet({"height": place + 2})

    @pl.when(z > 0)
    def _():
        greet({"height": place - 2})

    greet({"height": place + 1 - 2 * y})
    greet({"tm": 1 - side})
    for step in range(1, n_head):
        greet({"head": lax.rem(group + step, n_head)})

    def link(direction, slot, frame, cut):
        target = {
            UP: {"height": jnp.minimum(place + 2, n_height - 1)},
            DOWN: {"height": jnp.maximum(place - 2, 0)},
            ACROSS: {"height": place + 1 - 2 * y},
            CORE: {"tm": 1 - side},
        }[direction]
        landing = 2 if direction == CORE else frame
        span = pl.ds(ROW_CUTS[cut], ROW_CUTS[cut + 1] - ROW_CUTS[cut])
        return pltpu.make_async_remote_copy(
            src_ref=kv.at[slot, frame, span],
            dst_ref=kv.at[slot, landing, span],
            send_sem=send_sem.at[direction, slot, frame * CUTS + cut],
            recv_sem=recv_sem.at[slot, landing * CUTS + cut],
            device_id=target,
            device_id_type=MESH,
        )

    def on_line(d, sign):
        zs = z + sign * d
        real = (zs >= 0) & (zs < lines) & ((d > 0) | has_own)
        if sign > 0:
            real = real & (d > 0)
        proxied = (zs == last) & (y == 1)
        slot = jnp.clip(jnp.where(proxied, 2 * last, 2 * zs + y), 0, n_height - 1)
        up = real & (z < last) & ((sign < 0) | (d == 0))
        down = real & (z > 0) & ((sign > 0) | (d == 0))
        across = real & ((zs != last) | ((z == last) & (y == 0)))
        return real, slot, up, down, across

    def off_line(d, sign):
        zs = z + sign * d
        proxy = (z == last) & (y == 1) & (zs == last)
        real = (d >= 0) & (zs >= 0) & (zs < lines) & ((zs != last) | proxy)
        if sign > 0:
            real = real & (d > 0)
        slot = jnp.clip(2 * zs + 1 - y, 0, n_height - 1)
        return real, slot, proxy & real

    def act_on(flag, copy, act):
        @pl.when(flag)
        def _():
            getattr(copy, act)()

    def line_sends(d, act):
        sides = [on_line(d, -1), on_line(d, 1)]
        _, proxy_slot, proxy = off_line(0, -1)
        for frame in (0, 1):
            for cut in range(CUTS):
                for real, slot, up, down, across in sides:
                    if act == "start":
                        act_on(real & (d > 0), link(UP, slot, frame, cut), "wait_recv")
                    act_on(up, link(UP, slot, frame, cut), act)
                    act_on(down, link(DOWN, slot, frame, cut), act)
                    act_on(across, link(ACROSS, slot, frame, cut), act)
                    if frame == 0:
                        act_on(real, link(CORE, slot, 0, cut), act)
                now = proxy & (d == 1)
                if act == "start":
                    act_on(now, link(ACROSS, proxy_slot, frame, cut), "wait_recv")
                act_on(now, link(DOWN, proxy_slot, frame, cut), act)
                if frame == 0:
                    act_on(now, link(CORE, proxy_slot, 0, cut), act)

    def cross_sends(d, act):
        sides = [off_line(d, -1), off_line(d, 1)]
        for frame in (0, 1):
            for cut in range(CUTS):
                for real, slot, proxy in sides:
                    plain = real & jnp.logical_not(proxy)
                    if act == "start":
                        act_on(plain, link(ACROSS, slot, frame, cut), "wait_recv")
                    if frame == 0:
                        act_on(plain, link(CORE, slot, 0, cut), act)

    def far_weight(step):
        at = 2 * side + step
        first = pl.multiple_of(model - shared + at * far_width, HD)
        return pltpu.make_async_remote_copy(
            src_ref=w_hbm.at[:, pl.ds(first, far_width)],
            dst_ref=w_far.at[at],
            send_sem=far_send.at[step],
            recv_sem=far_recv.at[at],
            device_id={"head": 1 - group},
            device_id_type=MESH,
        )

    def pass_weight(step, owner):
        at = 2 * owner + step
        return pltpu.make_async_remote_copy(
            src_ref=w_far.at[at],
            dst_ref=w_far.at[at],
            send_sem=pass_send.at[step],
            recv_sem=far_recv.at[at],
            device_id={"tm": 1 - side},
            device_id_type=MESH,
        )

    def relay_weight(step):
        far_weight(step).wait_recv()
        pass_weight(step, side).start()

    factor = math.log2(math.e) / math.sqrt(HD)

    def attend(slot):
        for cut in range(CUTS):
            link(CORE, slot, 0, cut).wait_recv()
        for head in range(heads):
            lanes = slice(head * HD, (head + 1) * HD)
            query = q_ref[:, lanes]
            scores = []
            for frame in range(3):
                key = kv[slot, frame, 0:key_count, lanes]
                score = lax.dot_general(
                    query, key, (((1,), (1,)), ((), ())), preferred_element_type=jnp.float32
                )
                scores.append(score * factor + bias[...])
            largest = jnp.maximum(jnp.maximum(scores[0], scores[1]), scores[2])
            old_top = top[head]
            new_top = jnp.maximum(old_top, jnp.max(largest, axis=1, keepdims=True))
            alpha = jnp.exp2(old_top - new_top)
            top[head] = new_top
            added = None
            mixed = None
            for frame in range(3):
                weight = jnp.exp2(scores[frame] - new_top)
                value = kv[slot, frame, key_count : 2 * key_count, lanes]
                part = jnp.dot(
                    weight.astype(jnp.bfloat16), value, preferred_element_type=jnp.float32
                )
                added = weight if added is None else added + weight
                mixed = part if mixed is None else mixed + part
            total[head] = total[head] * alpha + added
            acc[head] = acc[head] * alpha + mixed

    own_copy.wait()
    for frame, held in ((0, 1 - side), (1, side)):
        for kind in range(2):
            for row in range(rows_dev):
                first = (kind * rows_dev + row) * VALID_COLS
                kv[place, frame, first : first + VALID_COLS, :] = own_raw[
                    kind, held, row, 0:VALID_COLS, :
                ]
    arrivals = (
        2 + (n_head - 1) + jnp.where(z < last, 1, 0) + jnp.where(z > 0, 1, 0)
    ).astype(jnp.int32)
    pl.semaphore_wait(barrier, arrivals)
    line_sends(0, "start")
    if shared:
        far_weight(0).start()
        far_weight(1).start()

    runs = 2 * rows_dev
    source = lax.broadcasted_iota(jnp.int32, (tokens, tokens), 1)
    wanted = lax.broadcasted_iota(jnp.int32, (tokens, tokens), 0)
    wanted = lax.rem(wanted, runs) * (tokens // runs) + lax.div(wanted, runs)
    moved = jnp.where(source == wanted, 1.0, 0.0).astype(jnp.bfloat16)
    q_ref[...] = jnp.dot(
        moved, raw_ref[...], preferred_element_type=jnp.float32
    ).astype(jnp.bfloat16)

    lane = lax.broadcasted_iota(jnp.int32, (tokens, key_count), 1)
    column = lax.rem(lane, VALID_COLS)
    right_half = lax.broadcasted_iota(jnp.int32, (tokens, key_count), 0) >= tokens // 2
    seen = jnp.where(right_half, column - TILE, (WINDOW * TILE - 1) - column) >= 0
    bias[...] = jnp.where(seen, 0.0, masked_value)
    top[...] = jnp.full_like(top, masked_value)
    total[...] = jnp.zeros_like(total)
    acc[...] = jnp.zeros_like(acc)

    def round_body(d, carry):
        if shared:

            @pl.when(d == 3)
            def _():
                relay_weight(0)

            @pl.when(d == lines + 1)
            def _():
                relay_weight(1)

        def one(j, inner):
            real = None
            sign_up = lax.rem(j, 2)
            line_m, line_p = on_line(d - 1, -1), on_line(d - 1, 1)
            off_m, off_p = off_line(d - 2, -1), off_line(d - 2, 1)
            first = j < 2
            real = jnp.where(
                first,
                jnp.where(sign_up == 0, line_m[0].astype(jnp.int32), line_p[0].astype(jnp.int32)),
                jnp.where(sign_up == 0, off_m[0].astype(jnp.int32), off_p[0].astype(jnp.int32)),
            )
            slot = jnp.where(
                first,
                jnp.where(sign_up == 0, line_m[1], line_p[1]),
                jnp.where(sign_up == 0, off_m[1], off_p[1]),
            )

            @pl.when(real == 1)
            def _():
                attend(slot)

            return inner

        lax.fori_loop(0, 4, one, 0)
        line_sends(d, "start")
        cross_sends(d - 1, "start")
        return carry

    lax.fori_loop(1, lines + 2, round_body, 0)

    for head in range(heads):
        whole = jnp.sum(total[head], axis=1, keepdims=True)
        att[:, head * HD : (head + 1) * HD] = (acc[head] / whole).astype(jnp.bfloat16)
    weight_copy.wait()

    def paired(value):
        return value.reshape(share // rows_dev, rows_dev, value.shape[1]).astype(jnp.bfloat16)

    def product(first_row, at):
        return jnp.dot(
            att[pl.ds(pl.multiple_of(first_row, share), share), :],
            w[:, pl.ds(pl.multiple_of(at * PIECE, PIECE), PIECE)],
            preferred_element_type=jnp.float32,
        ).astype(jnp.bfloat16)

    def parcel(step, at):
        return pltpu.make_async_remote_copy(
            src_ref=outbox.at[step - 1, at],
            dst_ref=inbox.at[step - 1, at],
            send_sem=part_send.at[step - 1, at],
            recv_sem=part_recv.at[step - 1, at],
            device_id={"head": lax.rem(group + step, n_head)},
            device_id_type=MESH,
        )

    if shared:
        far_rows = pl.ds(pl.multiple_of((1 - group) * share, share), share)
        att_copy = pltpu.make_async_remote_copy(
            src_ref=att.at[far_rows],
            dst_ref=att_far,
            send_sem=att_sems.at[0],
            recv_sem=att_sems.at[1],
            device_id={"head": 1 - group},
            device_id_type=MESH,
        )
        att_copy.start()

    for step in range(1, n_head):

        def ship(at, carry):
            outbox[step - 1, at] = product(lax.rem(group + step, n_head) * share, at)
            parcel(step, at).start()
            return carry

        lax.fori_loop(0, pieces, ship, 0)

    if shared:
        own_rows = pl.ds(pl.multiple_of(group * share, share), share)
        pass_weight(0, 1 - side).wait_recv()
        pass_weight(1, 1 - side).wait_recv()
        att_copy.wait_recv()
        for at in range(SHARED_CUTS):
            first = model - shared + at * far_width
            span = slice(first, first + far_width)
            near = jnp.dot(att[own_rows, :], w[:, span], preferred_element_type=jnp.float32)
            far = jnp.dot(att_far[...], w_far[at], preferred_element_type=jnp.float32)
            near = near.astype(jnp.bfloat16).astype(jnp.float32)
            far = far.astype(jnp.bfloat16).astype(jnp.float32)
            out_ref[:, :, span] = paired(near + far)

    def collect(at, carry):
        summed = product(group * share, at).astype(jnp.float32)
        for step in range(1, n_head):
            parcel(step, at).wait_recv()
            summed = summed + inbox[step - 1, at].astype(jnp.float32)
        out_ref[:, :, pl.ds(pl.multiple_of(at * PIECE, PIECE), PIECE)] = paired(summed)
        return carry

    lax.fori_loop(0, pieces, collect, 0)

    for step in range(1, n_head):

        def settle(at, carry):
            parcel(step, at).wait_send()
            return carry

        lax.fori_loop(0, pieces, settle, 0)

    if shared:
        att_copy.wait_send()
        for step in range(2):
            far_weight(step).wait_send()
            pass_weight(step, side).wait_send()

    def drain(d, carry):
        line_sends(d, "wait_send")
        cross_sends(d, "wait_send")
        return carry

    lax.fori_loop(0, lines, drain, 0)


def copy_kernel(in_ref, out_ref, held, sems):
    rows = in_ref.shape[0] // COPY_CUTS
    spans = [pl.ds(cut * rows, rows) for cut in range(COPY_CUTS)]
    loads, stores = [], []
    for cut, span in enumerate(spans):
        loads.append(pltpu.make_async_copy(in_ref.at[span], held.at[span], sems.at[0, cut]))
        stores.append(pltpu.make_async_copy(held.at[span], out_ref.at[span], sems.at[1, cut]))
        loads[cut].start()
    for load, store in zip(loads, stores):
        load.wait()
        store.start()
    for store in stores:
        store.wait()


def shared_width(n_head):
    return SHARED_PIECES * PIECE if n_head == 2 else 0


def on_device(n_height, n_head, queries, keys_values, out_weight):
    frames_dev, rows_dev, col_count, width = queries.shape
    model = out_weight.shape[1]
    heads = width // HD
    tokens = frames_dev * rows_dev * col_count
    key_count = rows_dev * VALID_COLS
    share = tokens // n_head
    shared = shared_width(n_head)
    far_width = shared // SHARED_CUTS
    pieces = (model - shared) // PIECE
    assert frames_dev == 2 and rows_dev == PAD_ROWS and col_count == 4 * TILE
    assert n_height % 2 == 0 and n_height * rows_dev <= WINDOW * TILE
    raw = queries.reshape(tokens, width)
    others = n_head - 1
    out = pl.pallas_call(
        functools.partial(kernel, n_height, n_head, rows_dev),
        out_shape=jax.ShapeDtypeStruct((share // rows_dev, rows_dev, model), jnp.bfloat16),
        in_specs=[
            pl.BlockSpec(memory_space=pltpu.VMEM),
            pl.BlockSpec(memory_space=pl.ANY),
            pl.BlockSpec(memory_space=pl.ANY),
        ],
        out_specs=pl.BlockSpec(memory_space=pltpu.VMEM),
        scratch_shapes=[
            pltpu.VMEM((n_height, 3, 2 * key_count, width), jnp.bfloat16),
            pltpu.VMEM((width, model), jnp.bfloat16),
            pltpu.VMEM((tokens, key_count), jnp.float32),
            pltpu.VMEM((heads, tokens, 1), jnp.float32),
            pltpu.VMEM((heads, tokens, key_count), jnp.float32),
            pltpu.VMEM((heads, tokens, HD), jnp.float32),
            pltpu.VMEM((tokens, width), jnp.bfloat16),
            pltpu.VMEM((others, pieces, share, PIECE), jnp.bfloat16),
            pltpu.VMEM((others, pieces, share, PIECE), jnp.bfloat16),
            pltpu.SemaphoreType.DMA,
            pltpu.SemaphoreType.DMA,
            pltpu.SemaphoreType.DMA((4, n_height, 2 * CUTS)),
            pltpu.SemaphoreType.DMA((n_height, 3 * CUTS)),
            pltpu.SemaphoreType.DMA((others, pieces)),
            pltpu.SemaphoreType.DMA((others, pieces)),
            pltpu.VMEM((SHARED_CUTS, width, max(far_width, HD)), jnp.bfloat16),
            pltpu.VMEM((share, width), jnp.bfloat16),
            pltpu.SemaphoreType.DMA((2,)),
            pltpu.SemaphoreType.DMA((2,)),
            pltpu.SemaphoreType.DMA((SHARED_CUTS,)),
            pltpu.SemaphoreType.DMA((2,)),
            pltpu.VMEM((tokens, width), jnp.bfloat16),
            pltpu.VMEM(keys_values.shape, jnp.bfloat16),
        ],
        compiler_params=pltpu.CompilerParams(
            collective_id=0, has_side_effects=True, vmem_limit_bytes=56 * 2**20
        ),
        name="tile_attention",
    )(raw, keys_values, out_weight)
    out = pl.pallas_call(
        copy_kernel,
        out_shape=jax.ShapeDtypeStruct(out.shape, out.dtype),
        in_specs=[pl.BlockSpec(memory_space=pl.ANY)],
        out_specs=pl.BlockSpec(memory_space=pl.ANY),
        scratch_shapes=[
            pltpu.VMEM(out.shape, out.dtype),
            pltpu.SemaphoreType.DMA((2, COPY_CUTS)),
        ],
        name="hand_over",
    )(out)
    return out.reshape(col_count // n_head, frames_dev, rows_dev, model)


def solution(mesh):
    placed = (
        P("tm", "height", None, "head"),
        P(None, "tm", "height", None, "head"),
        P("head", None),
    )
    return jax.shard_map(
        functools.partial(on_device, mesh.shape["height"], mesh.shape["head"]),
        mesh=mesh,
        in_specs=placed,
        out_specs=P("head", "tm", "height", None),
        check_vma=False,
    )
```

```python
import functools
import math

import jax
import jax.numpy as jnp
from jax import lax
from jax.experimental import pallas as pl
from jax.experimental.pallas import tpu as pltpu
from jax.sharding import PartitionSpec as P

HD = 128
TILE = 16
WINDOW = 3
PAD_ROWS = 2
VALID_COLS = 52
MESH = pl.DeviceIdType.MESH
UP, DOWN, ACROSS, CORE = 0, 1, 2, 3
PIECE = 512
ROW_CUTS = (0, 208)
CUTS = len(ROW_CUTS) - 1
SHARED_PIECES = 6
SHARED_CUTS = 4
COPY_CUTS = 4

masked_value = -1e30


def kernel(
    n_height,
    n_head,
    rows_dev,
    raw_ref,
    kv_hbm,
    w_hbm,
    out_ref,
    kv,
    w,
    bias,
    top,
    total,
    acc,
    att,
    outbox,
    inbox,
    own_sem,
    w_sem,
    send_sem,
    recv_sem,
    part_send,
    part_recv,
    w_far,
    att_far,
    far_send,
    pass_send,
    far_recv,
    att_sems,
    q_ref,
    own_raw,
):
    lines = n_height // 2
    tokens, width = raw_ref.shape
    heads = width // HD
    key_count = rows_dev * VALID_COLS
    model = w.shape[1]
    shared = shared_width(n_head)
    far_width = shared // SHARED_CUTS
    pieces = (model - shared) // PIECE
    share = tokens // n_head
    last = lines - 1

    side = lax.axis_index("tm")
    place = lax.axis_index("height")
    group = lax.axis_index("head")
    z = place // 2
    y = place % 2
    has_own = place < n_height - 1

    weight_copy = pltpu.make_async_copy(w_hbm, w, w_sem)
    weight_copy.start()
    own_copy = pltpu.make_async_copy(kv_hbm, own_raw, own_sem)
    own_copy.start()

    barrier = pltpu.get_barrier_semaphore()

    def greet(target):
        pl.semaphore_signal(barrier, inc=1, device_id=target, device_id_type=MESH)

    @pl.when(z < last)
    def _():
        greet({"height": place + 2})

    @pl.when(z > 0)
    def _():
        greet({"height": place - 2})

    greet({"height": place + 1 - 2 * y})
    greet({"tm": 1 - side})
    for step in range(1, n_head):
        greet({"head": lax.rem(group + step, n_head)})

    def link(direction, slot, frame, cut):
        target = {
            UP: {"height": jnp.minimum(place + 2, n_height - 1)},
            DOWN: {"height": jnp.maximum(place - 2, 0)},
            ACROSS: {"height": place + 1 - 2 * y},
            CORE: {"tm": 1 - side},
        }[direction]
        landing = 2 if direction == CORE else frame
        span = pl.ds(ROW_CUTS[cut], ROW_CUTS[cut + 1] - ROW_CUTS[cut])
        return pltpu.make_async_remote_copy(
            src_ref=kv.at[slot, frame, span],
            dst_ref=kv.at[slot, landing, span],
            send_sem=send_sem.at[direction, slot, frame * CUTS + cut],
            recv_sem=recv_sem.at[slot, landing * CUTS + cut],
            device_id=target,
            device_id_type=MESH,
        )

    def on_line(d, sign):
        zs = z + sign * d
        real = (zs >= 0) & (zs < lines) & ((d > 0) | has_own)
        if sign > 0:
            real = real & (d > 0)
        proxied = (zs == last) & (y == 1)
        slot = jnp.clip(jnp.where(proxied, 2 * last, 2 * zs + y), 0, n_height - 1)
        up = real & (z < last) & ((sign < 0) | (d == 0))
        down = real & (z > 0) & ((sign > 0) | (d == 0))
        across = real & ((zs != last) | ((z == last) & (y == 0)))
        whole = across & ((zs != 0) | (z == 0) | (y == 1))
        return real, slot, up, down, (across, whole)

    def off_line(d, sign):
        zs = z + sign * d
        proxy = (z == last) & (y == 1) & (zs == last)
        real = (d >= 0) & (zs >= 0) & (zs < lines) & ((zs != last) | proxy)
        if sign > 0:
            real = real & (d > 0)
        slot = jnp.clip(2 * zs + 1 - y, 0, n_height - 1)
        climbs = real & (zs == 0) & (y == 1) & (z < last)
        return real, slot, proxy & real, climbs

    def act_on(flag, copy, act):
        @pl.when(flag)
        def _():
            getattr(copy, act)()

    def line_sends(d, act):
        sides = [on_line(d, -1), on_line(d, 1)]
        _, proxy_slot, proxy, _ = off_line(0, -1)
        for frame in (0, 1):
            for cut in range(CUTS):
                for real, slot, up, down, across in sides:
                    if act == "start":
                        act_on(real & (d > 0), link(UP, slot, frame, cut), "wait_recv")
                    act_on(up, link(UP, slot, frame, cut), act)
                    act_on(down, link(DOWN, slot, frame, cut), act)
                    act_on(across[frame], link(ACROSS, slot, frame, cut), act)
                    if frame == 0:
                        act_on(real, link(CORE, slot, 0, cut), act)
                now = proxy & (d == 1)
                if act == "start":
                    act_on(now, link(ACROSS, proxy_slot, frame, cut), "wait_recv")
                act_on(now, link(DOWN, proxy_slot, frame, cut), act)
                if frame == 0:
                    act_on(now, link(CORE, proxy_slot, 0, cut), act)

    def cross_sends(d, act):
        sides = [off_line(d, -1), off_line(d, 1)]
        for frame in (0, 1):
            for cut in range(CUTS):
                for real, slot, proxy, climbs in sides:
                    plain = real & jnp.logical_not(proxy)
                    if act == "start":
                        act_on(plain, link(ACROSS, slot, frame, cut), "wait_recv")
                    if frame == 1:
                        act_on(climbs, link(UP, slot, frame, cut), act)
                    if frame == 0:
                        act_on(plain, link(CORE, slot, 0, cut), act)

    def far_weight(step):
        at = 2 * side + step
        first = pl.multiple_of(model - shared + at * far_width, HD)
        return pltpu.make_async_remote_copy(
            src_ref=w_hbm.at[:, pl.ds(first, far_width)],
            dst_ref=w_far.at[at],
            send_sem=far_send.at[step],
            recv_sem=far_recv.at[at],
            device_id={"head": 1 - group},
            device_id_type=MESH,
        )

    def pass_weight(step, owner):
        at = 2 * owner + step
        return pltpu.make_async_remote_copy(
            src_ref=w_far.at[at],
            dst_ref=w_far.at[at],
            send_sem=pass_send.at[step],
            recv_sem=far_recv.at[at],
            device_id={"tm": 1 - side},
            device_id_type=MESH,
        )

    def relay_weight(step):
        far_weight(step).wait_recv()
        pass_weight(step, side).start()

    factor = math.log2(math.e) / math.sqrt(HD)

    def attend(slot):
        for cut in range(CUTS):
            link(CORE, slot, 0, cut).wait_recv()
        for head in range(heads):
            lanes = slice(head * HD, (head + 1) * HD)
            query = q_ref[:, lanes]
            scores = []
            for frame in range(3):
                key = kv[slot, frame, 0:key_count, lanes]
                score = lax.dot_general(
                    query, key, (((1,), (1,)), ((), ())), preferred_element_type=jnp.float32
                )
                scores.append(score * factor + bias[...])
            largest = jnp.maximum(jnp.maximum(scores[0], scores[1]), scores[2])
            old_top = top[head]
            new_top = jnp.maximum(old_top, jnp.max(largest, axis=1, keepdims=True))
            alpha = jnp.exp2(old_top - new_top)
            top[head] = new_top
            added = None
            mixed = None
            for frame in range(3):
                weight = jnp.exp2(scores[frame] - new_top)
                value = kv[slot, frame, key_count : 2 * key_count, lanes]
                part = jnp.dot(
                    weight.astype(jnp.bfloat16), value, preferred_element_type=jnp.float32
                )
                added = weight if added is None else added + weight
                mixed = part if mixed is None else mixed + part
            total[head] = total[head] * alpha + added
            acc[head] = acc[head] * alpha + mixed

    own_copy.wait()
    for frame, held in ((0, 1 - side), (1, side)):
        for kind in range(2):
            for row in range(rows_dev):
                first = (kind * rows_dev + row) * VALID_COLS
                kv[place, frame, first : first + VALID_COLS, :] = own_raw[
                    kind, held, row, 0:VALID_COLS, :
                ]
    arrivals = (
        2 + (n_head - 1) + jnp.where(z < last, 1, 0) + jnp.where(z > 0, 1, 0)
    ).astype(jnp.int32)
    pl.semaphore_wait(barrier, arrivals)
    line_sends(0, "start")
    if shared:
        far_weight(0).start()
        far_weight(1).start()

    runs = 2 * rows_dev
    source = lax.broadcasted_iota(jnp.int32, (tokens, tokens), 1)
    wanted = lax.broadcasted_iota(jnp.int32, (tokens, tokens), 0)
    wanted = lax.rem(wanted, runs) * (tokens // runs) + lax.div(wanted, runs)
    moved = jnp.where(source == wanted, 1.0, 0.0).astype(jnp.bfloat16)
    q_ref[...] = jnp.dot(
        moved, raw_ref[...], preferred_element_type=jnp.float32
    ).astype(jnp.bfloat16)

    lane = lax.broadcasted_iota(jnp.int32, (tokens, key_count), 1)
    column = lax.rem(lane, VALID_COLS)
    right_half = lax.broadcasted_iota(jnp.int32, (tokens, key_count), 0) >= tokens // 2
    seen = jnp.where(right_half, column - TILE, (WINDOW * TILE - 1) - column) >= 0
    bias[...] = jnp.where(seen, 0.0, masked_value)
    top[...] = jnp.full_like(top, masked_value)
    total[...] = jnp.zeros_like(total)
    acc[...] = jnp.zeros_like(acc)

    def round_body(d, carry):
        if shared:

            @pl.when(d == 3)
            def _():
                relay_weight(0)

            @pl.when(d == lines + 1)
            def _():
                relay_weight(1)

        def one(j, inner):
            real = None
            sign_up = lax.rem(j, 2)
            line_m, line_p = on_line(d - 1, -1), on_line(d - 1, 1)
            off_m, off_p = off_line(d - 2, -1), off_line(d - 2, 1)
            first = j < 2
            real = jnp.where(
                first,
                jnp.where(sign_up == 0, line_m[0].astype(jnp.int32), line_p[0].astype(jnp.int32)),
                jnp.where(sign_up == 0, off_m[0].astype(jnp.int32), off_p[0].astype(jnp.int32)),
            )
            slot = jnp.where(
                first,
                jnp.where(sign_up == 0, line_m[1], line_p[1]),
                jnp.where(sign_up == 0, off_m[1], off_p[1]),
            )

            @pl.when(real == 1)
            def _():
                attend(slot)

            return inner

        lax.fori_loop(0, 4, one, 0)
        line_sends(d, "start")
        cross_sends(d - 1, "start")
        return carry

    lax.fori_loop(1, lines + 2, round_body, 0)

    for head in range(heads):
        whole = jnp.sum(total[head], axis=1, keepdims=True)
        att[:, head * HD : (head + 1) * HD] = (acc[head] / whole).astype(jnp.bfloat16)
    weight_copy.wait()

    def paired(value):
        return value.reshape(share // rows_dev, rows_dev, value.shape[1]).astype(jnp.bfloat16)

    def product(first_row, at):
        return jnp.dot(
            att[pl.ds(pl.multiple_of(first_row, share), share), :],
            w[:, pl.ds(pl.multiple_of(at * PIECE, PIECE), PIECE)],
            preferred_element_type=jnp.float32,
        ).astype(jnp.bfloat16)

    def parcel(step, at):
        return pltpu.make_async_remote_copy(
            src_ref=outbox.at[step - 1, at],
            dst_ref=inbox.at[step - 1, at],
            send_sem=part_send.at[step - 1, at],
            recv_sem=part_recv.at[step - 1, at],
            device_id={"head": lax.rem(group + step, n_head)},
            device_id_type=MESH,
        )

    if shared:
        far_rows = pl.ds(pl.multiple_of((1 - group) * share, share), share)
        att_copy = pltpu.make_async_remote_copy(
            src_ref=att.at[far_rows],
            dst_ref=att_far,
            send_sem=att_sems.at[0],
            recv_sem=att_sems.at[1],
            device_id={"head": 1 - group},
            device_id_type=MESH,
        )
        att_copy.start()

    for step in range(1, n_head):

        def ship(at, carry):
            outbox[step - 1, at] = product(lax.rem(group + step, n_head) * share, at)
            parcel(step, at).start()
            return carry

        lax.fori_loop(0, pieces, ship, 0)

    if shared:
        own_rows = pl.ds(pl.multiple_of(group * share, share), share)
        pass_weight(0, 1 - side).wait_recv()
        pass_weight(1, 1 - side).wait_recv()
        att_copy.wait_recv()
        for at in range(SHARED_CUTS):
            first = model - shared + at * far_width
            span = slice(first, first + far_width)
            near = jnp.dot(att[own_rows, :], w[:, span], preferred_element_type=jnp.float32)
            far = jnp.dot(att_far[...], w_far[at], preferred_element_type=jnp.float32)
            near = near.astype(jnp.bfloat16).astype(jnp.float32)
            far = far.astype(jnp.bfloat16).astype(jnp.float32)
            out_ref[:, :, span] = paired(near + far)

    def collect(at, carry):
        summed = product(group * share, at).astype(jnp.float32)
        for step in range(1, n_head):
            parcel(step, at).wait_recv()
            summed = summed + inbox[step - 1, at].astype(jnp.float32)
        out_ref[:, :, pl.ds(pl.multiple_of(at * PIECE, PIECE), PIECE)] = paired(summed)
        return carry

    lax.fori_loop(0, pieces, collect, 0)

    for step in range(1, n_head):

        def settle(at, carry):
            parcel(step, at).wait_send()
            return carry

        lax.fori_loop(0, pieces, settle, 0)

    if shared:
        att_copy.wait_send()
        for step in range(2):
            far_weight(step).wait_send()
            pass_weight(step, side).wait_send()

    def drain(d, carry):
        line_sends(d, "wait_send")
        cross_sends(d, "wait_send")
        return carry

    lax.fori_loop(0, lines, drain, 0)


def copy_kernel(in_ref, out_ref, held, sems):
    rows = in_ref.shape[0] // COPY_CUTS
    spans = [pl.ds(cut * rows, rows) for cut in range(COPY_CUTS)]
    loads, stores = [], []
    for cut, span in enumerate(spans):
        loads.append(pltpu.make_async_copy(in_ref.at[span], held.at[span], sems.at[0, cut]))
        stores.append(pltpu.make_async_copy(held.at[span], out_ref.at[span], sems.at[1, cut]))
        loads[cut].start()
    for load, store in zip(loads, stores):
        load.wait()
        store.start()
    for store in stores:
        store.wait()


def shared_width(n_head):
    return SHARED_PIECES * PIECE if n_head == 2 else 0


def on_device(n_height, n_head, queries, keys_values, out_weight):
    frames_dev, rows_dev, col_count, width = queries.shape
    model = out_weight.shape[1]
    heads = width // HD
    tokens = frames_dev * rows_dev * col_count
    key_count = rows_dev * VALID_COLS
    share = tokens // n_head
    shared = shared_width(n_head)
    far_width = shared // SHARED_CUTS
    pieces = (model - shared) // PIECE
    assert frames_dev == 2 and rows_dev == PAD_ROWS and col_count == 4 * TILE
    assert n_height % 2 == 0 and n_height * rows_dev <= WINDOW * TILE
    raw = queries.reshape(tokens, width)
    others = n_head - 1
    out = pl.pallas_call(
        functools.partial(kernel, n_height, n_head, rows_dev),
        out_shape=jax.ShapeDtypeStruct((share // rows_dev, rows_dev, model), jnp.bfloat16),
        in_specs=[
            pl.BlockSpec(memory_space=pltpu.VMEM),
            pl.BlockSpec(memory_space=pl.ANY),
            pl.BlockSpec(memory_space=pl.ANY),
        ],
        out_specs=pl.BlockSpec(memory_space=pltpu.VMEM),
        scratch_shapes=[
            pltpu.VMEM((n_height, 3, 2 * key_count, width), jnp.bfloat16),
            pltpu.VMEM((width, model), jnp.bfloat16),
            pltpu.VMEM((tokens, key_count), jnp.float32),
            pltpu.VMEM((heads, tokens, 1), jnp.float32),
            pltpu.VMEM((heads, tokens, key_count), jnp.float32),
            pltpu.VMEM((heads, tokens, HD), jnp.float32),
            pltpu.VMEM((tokens, width), jnp.bfloat16),
            pltpu.VMEM((others, pieces, share, PIECE), jnp.bfloat16),
            pltpu.VMEM((others, pieces, share, PIECE), jnp.bfloat16),
            pltpu.SemaphoreType.DMA,
            pltpu.SemaphoreType.DMA,
            pltpu.SemaphoreType.DMA((4, n_height, 2 * CUTS)),
            pltpu.SemaphoreType.DMA((n_height, 3 * CUTS)),
            pltpu.SemaphoreType.DMA((others, pieces)),
            pltpu.SemaphoreType.DMA((others, pieces)),
            pltpu.VMEM((SHARED_CUTS, width, max(far_width, HD)), jnp.bfloat16),
            pltpu.VMEM((share, width), jnp.bfloat16),
            pltpu.SemaphoreType.DMA((2,)),
            pltpu.SemaphoreType.DMA((2,)),
            pltpu.SemaphoreType.DMA((SHARED_CUTS,)),
            pltpu.SemaphoreType.DMA((2,)),
            pltpu.VMEM((tokens, width), jnp.bfloat16),
            pltpu.VMEM(keys_values.shape, jnp.bfloat16),
        ],
        compiler_params=pltpu.CompilerParams(
            collective_id=0, has_side_effects=True, vmem_limit_bytes=56 * 2**20
        ),
        name="tile_attention",
    )(raw, keys_values, out_weight)
    out = pl.pallas_call(
        copy_kernel,
        out_shape=jax.ShapeDtypeStruct(out.shape, out.dtype),
        in_specs=[pl.BlockSpec(memory_space=pl.ANY)],
        out_specs=pl.BlockSpec(memory_space=pl.ANY),
        scratch_shapes=[
            pltpu.VMEM(out.shape, out.dtype),
            pltpu.SemaphoreType.DMA((2, COPY_CUTS)),
        ],
        name="hand_over",
    )(out)
    return out.reshape(col_count // n_head, frames_dev, rows_dev, model)


def solution(mesh):
    placed = (
        P("tm", "height", None, "head"),
        P(None, "tm", "height", None, "head"),
        P("head", None),
    )
    return jax.shard_map(
        functools.partial(on_device, mesh.shape["height"], mesh.shape["head"]),
        mesh=mesh,
        in_specs=placed,
        out_specs=P("head", "tm", "height", None),
        check_vma=False,
    )
```

```python
import functools
import math

import jax
import jax.numpy as jnp
from jax import lax
from jax.experimental import pallas as pl
from jax.experimental.pallas import tpu as pltpu
from jax.sharding import PartitionSpec as P

HD = 128
TILE = 16
WINDOW = 3
PAD_ROWS = 2
VALID_COLS = 52
MESH = pl.DeviceIdType.MESH
UP, DOWN, ACROSS, CORE = 0, 1, 2, 3
PIECE = 512
ROW_CUTS = (0, 208)
CUTS = len(ROW_CUTS) - 1
SHARED_PIECES = 6
SHARED_CUTS = 4

masked_value = -1e30


def kernel(
    n_height,
    n_head,
    rows_dev,
    raw_ref,
    kv_hbm,
    w_hbm,
    out_ref,
    kv,
    w,
    bias,
    top,
    total,
    acc,
    att,
    outbox,
    inbox,
    own_sem,
    w_sem,
    send_sem,
    recv_sem,
    part_send,
    part_recv,
    w_far,
    att_far,
    far_send,
    pass_send,
    far_recv,
    att_sems,
    q_ref,
    own_raw,
):
    lines = n_height // 2
    tokens, width = raw_ref.shape
    heads = width // HD
    key_count = rows_dev * VALID_COLS
    model = w.shape[1]
    shared = shared_width(n_head)
    far_width = shared // SHARED_CUTS
    pieces = (model - shared) // PIECE
    share = tokens // n_head
    last = lines - 1

    side = lax.axis_index("tm")
    place = lax.axis_index("height")
    group = lax.axis_index("head")
    z = place // 2
    y = place % 2
    has_own = place < n_height - 1

    weight_copy = pltpu.make_async_copy(w_hbm, w, w_sem)
    weight_copy.start()
    own_copy = pltpu.make_async_copy(kv_hbm, own_raw, own_sem)
    own_copy.start()

    barrier = pltpu.get_barrier_semaphore()

    def greet(target):
        pl.semaphore_signal(barrier, inc=1, device_id=target, device_id_type=MESH)

    @pl.when(z < last)
    def _():
        greet({"height": place + 2})

    @pl.when(z > 0)
    def _():
        greet({"height": place - 2})

    greet({"height": place + 1 - 2 * y})
    greet({"tm": 1 - side})
    for step in range(1, n_head):
        greet({"head": lax.rem(group + step, n_head)})

    def link(direction, slot, frame, cut):
        target = {
            UP: {"height": jnp.minimum(place + 2, n_height - 1)},
            DOWN: {"height": jnp.maximum(place - 2, 0)},
            ACROSS: {"height": place + 1 - 2 * y},
            CORE: {"tm": 1 - side},
        }[direction]
        landing = 2 if direction == CORE else frame
        span = pl.ds(ROW_CUTS[cut], ROW_CUTS[cut + 1] - ROW_CUTS[cut])
        return pltpu.make_async_remote_copy(
            src_ref=kv.at[slot, frame, span],
            dst_ref=kv.at[slot, landing, span],
            send_sem=send_sem.at[direction, slot, frame * CUTS + cut],
            recv_sem=recv_sem.at[slot, landing * CUTS + cut],
            device_id=target,
            device_id_type=MESH,
        )

    def on_line(d, sign):
        zs = z + sign * d
        real = (zs >= 0) & (zs < lines) & ((d > 0) | has_own)
        if sign > 0:
            real = real & (d > 0)
        proxied = (zs == last) & (y == 1)
        slot = jnp.clip(jnp.where(proxied, 2 * last, 2 * zs + y), 0, n_height - 1)
        up = real & (z < last) & ((sign < 0) | (d == 0))
        down = real & (z > 0) & ((sign > 0) | (d == 0))
        across = real & ((zs != last) | ((z == last) & (y == 0)))
        whole = across & ((zs != 0) | (z == 0) | (y == 1))
        return real, slot, up, down, (across, whole)

    def off_line(d, sign):
        zs = z + sign * d
        proxy = (z == last) & (y == 1) & (zs == last)
        real = (d >= 0) & (zs >= 0) & (zs < lines) & ((zs != last) | proxy)
        if sign > 0:
            real = real & (d > 0)
        slot = jnp.clip(2 * zs + 1 - y, 0, n_height - 1)
        climbs = real & (zs == 0) & (y == 1) & (z < last)
        return real, slot, proxy & real, climbs

    def act_on(flag, copy, act):
        @pl.when(flag)
        def _():
            getattr(copy, act)()

    def line_sends(d, act):
        sides = [on_line(d, -1), on_line(d, 1)]
        _, proxy_slot, proxy, _ = off_line(0, -1)
        for frame in (0, 1):
            for cut in range(CUTS):
                for real, slot, up, down, across in sides:
                    if act == "start":
                        act_on(real & (d > 0), link(UP, slot, frame, cut), "wait_recv")
                    act_on(up, link(UP, slot, frame, cut), act)
                    act_on(down, link(DOWN, slot, frame, cut), act)
                    act_on(across[frame], link(ACROSS, slot, frame, cut), act)
                    if frame == 0:
                        act_on(real, link(CORE, slot, 0, cut), act)
                now = proxy & (d == 1)
                if act == "start":
                    act_on(now, link(ACROSS, proxy_slot, frame, cut), "wait_recv")
                act_on(now, link(DOWN, proxy_slot, frame, cut), act)
                if frame == 0:
                    act_on(now, link(CORE, proxy_slot, 0, cut), act)

    def cross_sends(d, act):
        sides = [off_line(d, -1), off_line(d, 1)]
        for frame in (0, 1):
            for cut in range(CUTS):
                for real, slot, proxy, climbs in sides:
                    plain = real & jnp.logical_not(proxy)
                    if act == "start":
                        act_on(plain, link(ACROSS, slot, frame, cut), "wait_recv")
                    if frame == 1:
                        act_on(climbs, link(UP, slot, frame, cut), act)
                    if frame == 0:
                        act_on(plain, link(CORE, slot, 0, cut), act)

    def far_weight(step):
        at = 2 * side + step
        first = pl.multiple_of(model - shared + at * far_width, HD)
        return pltpu.make_async_remote_copy(
            src_ref=w_hbm.at[:, pl.ds(first, far_width)],
            dst_ref=w_far.at[at],
            send_sem=far_send.at[step],
            recv_sem=far_recv.at[at],
            device_id={"head": 1 - group},
            device_id_type=MESH,
        )

    def pass_weight(step, owner):
        at = 2 * owner + step
        return pltpu.make_async_remote_copy(
            src_ref=w_far.at[at],
            dst_ref=w_far.at[at],
            send_sem=pass_send.at[step],
            recv_sem=far_recv.at[at],
            device_id={"tm": 1 - side},
            device_id_type=MESH,
        )

    def relay_weight(step):
        far_weight(step).wait_recv()
        pass_weight(step, side).start()

    factor = math.log2(math.e) / math.sqrt(HD)

    def attend(slot):
        for cut in range(CUTS):
            link(CORE, slot, 0, cut).wait_recv()
        for head in range(heads):
            lanes = slice(head * HD, (head + 1) * HD)
            query = q_ref[:, lanes]
            scores = []
            for frame in range(3):
                key = kv[slot, frame, 0:key_count, lanes]
                score = lax.dot_general(
                    query, key, (((1,), (1,)), ((), ())), preferred_element_type=jnp.float32
                )
                scores.append(score * factor + bias[...])
            largest = jnp.maximum(jnp.maximum(scores[0], scores[1]), scores[2])
            old_top = top[head]
            new_top = jnp.maximum(old_top, jnp.max(largest, axis=1, keepdims=True))
            alpha = jnp.exp2(old_top - new_top)
            top[head] = new_top
            added = None
            mixed = None
            for frame in range(3):
                weight = jnp.exp2(scores[frame] - new_top)
                value = kv[slot, frame, key_count : 2 * key_count, lanes]
                part = jnp.dot(
                    weight.astype(jnp.bfloat16), value, preferred_element_type=jnp.float32
                )
                added = weight if added is None else added + weight
                mixed = part if mixed is None else mixed + part
            total[head] = total[head] * alpha + added
            acc[head] = acc[head] * alpha + mixed

    own_copy.wait()
    for frame, held in ((0, 1 - side), (1, side)):
        for kind in range(2):
            for row in range(rows_dev):
                first = (kind * rows_dev + row) * VALID_COLS
                kv[place, frame, first : first + VALID_COLS, :] = own_raw[
                    kind, held, row, 0:VALID_COLS, :
                ]
    arrivals = (
        2 + (n_head - 1) + jnp.where(z < last, 1, 0) + jnp.where(z > 0, 1, 0)
    ).astype(jnp.int32)
    pl.semaphore_wait(barrier, arrivals)
    line_sends(0, "start")
    if shared:
        far_weight(0).start()
        far_weight(1).start()

    runs = 2 * rows_dev
    source = lax.broadcasted_iota(jnp.int32, (tokens, tokens), 1)
    wanted = lax.broadcasted_iota(jnp.int32, (tokens, tokens), 0)
    wanted = lax.rem(wanted, runs) * (tokens // runs) + lax.div(wanted, runs)
    moved = jnp.where(source == wanted, 1.0, 0.0).astype(jnp.bfloat16)
    q_ref[...] = jnp.dot(
        moved, raw_ref[...], preferred_element_type=jnp.float32
    ).astype(jnp.bfloat16)

    lane = lax.broadcasted_iota(jnp.int32, (tokens, key_count), 1)
    column = lax.rem(lane, VALID_COLS)
    right_half = lax.broadcasted_iota(jnp.int32, (tokens, key_count), 0) >= tokens // 2
    seen = jnp.where(right_half, column - TILE, (WINDOW * TILE - 1) - column) >= 0
    bias[...] = jnp.where(seen, 0.0, masked_value)
    top[...] = jnp.full_like(top, masked_value)
    total[...] = jnp.zeros_like(total)
    acc[...] = jnp.zeros_like(acc)

    def round_body(d, carry):
        if shared:

            @pl.when(d == 3)
            def _():
                relay_weight(0)

            @pl.when(d == lines + 1)
            def _():
                relay_weight(1)

        def one(j, inner):
            real = None
            sign_up = lax.rem(j, 2)
            line_m, line_p = on_line(d - 1, -1), on_line(d - 1, 1)
            off_m, off_p = off_line(d - 2, -1), off_line(d - 2, 1)
            first = j < 2
            real = jnp.where(
                first,
                jnp.where(sign_up == 0, line_m[0].astype(jnp.int32), line_p[0].astype(jnp.int32)),
                jnp.where(sign_up == 0, off_m[0].astype(jnp.int32), off_p[0].astype(jnp.int32)),
            )
            slot = jnp.where(
                first,
                jnp.where(sign_up == 0, line_m[1], line_p[1]),
                jnp.where(sign_up == 0, off_m[1], off_p[1]),
            )

            @pl.when(real == 1)
            def _():
                attend(slot)

            return inner

        lax.fori_loop(0, 4, one, 0)
        line_sends(d, "start")
        cross_sends(d - 1, "start")
        return carry

    lax.fori_loop(1, lines + 2, round_body, 0)

    for head in range(heads):
        whole = jnp.sum(total[head], axis=1, keepdims=True)
        att[:, head * HD : (head + 1) * HD] = (acc[head] / whole).astype(jnp.bfloat16)
    weight_copy.wait()

    def paired(value):
        return value.reshape(share // rows_dev, rows_dev, value.shape[1]).astype(jnp.bfloat16)

    def product(first_row, at):
        return jnp.dot(
            att[pl.ds(pl.multiple_of(first_row, share), share), :],
            w[:, pl.ds(pl.multiple_of(at * PIECE, PIECE), PIECE)],
            preferred_element_type=jnp.float32,
        ).astype(jnp.bfloat16)

    def parcel(step, at):
        return pltpu.make_async_remote_copy(
            src_ref=outbox.at[step - 1, at],
            dst_ref=inbox.at[step - 1, at],
            send_sem=part_send.at[step - 1, at],
            recv_sem=part_recv.at[step - 1, at],
            device_id={"head": lax.rem(group + step, n_head)},
            device_id_type=MESH,
        )

    if shared:
        far_rows = pl.ds(pl.multiple_of((1 - group) * share, share), share)
        att_copy = pltpu.make_async_remote_copy(
            src_ref=att.at[far_rows],
            dst_ref=att_far,
            send_sem=att_sems.at[0],
            recv_sem=att_sems.at[1],
            device_id={"head": 1 - group},
            device_id_type=MESH,
        )
        att_copy.start()

    for step in range(1, n_head):

        def ship(at, carry):
            outbox[step - 1, at] = product(lax.rem(group + step, n_head) * share, at)
            parcel(step, at).start()
            return carry

        lax.fori_loop(0, pieces, ship, 0)

    if shared:
        own_rows = pl.ds(pl.multiple_of(group * share, share), share)
        pass_weight(0, 1 - side).wait_recv()
        pass_weight(1, 1 - side).wait_recv()
        att_copy.wait_recv()
        for at in range(SHARED_CUTS):
            first = model - shared + at * far_width
            span = slice(first, first + far_width)
            near = jnp.dot(att[own_rows, :], w[:, span], preferred_element_type=jnp.float32)
            far = jnp.dot(att_far[...], w_far[at], preferred_element_type=jnp.float32)
            near = near.astype(jnp.bfloat16).astype(jnp.float32)
            far = far.astype(jnp.bfloat16).astype(jnp.float32)
            out_ref[:, :, span] = paired(near + far)

    def collect(at, carry):
        summed = product(group * share, at).astype(jnp.float32)
        for step in range(1, n_head):
            parcel(step, at).wait_recv()
            summed = summed + inbox[step - 1, at].astype(jnp.float32)
        out_ref[:, :, pl.ds(pl.multiple_of(at * PIECE, PIECE), PIECE)] = paired(summed)
        return carry

    lax.fori_loop(0, pieces, collect, 0)

    for step in range(1, n_head):

        def settle(at, carry):
            parcel(step, at).wait_send()
            return carry

        lax.fori_loop(0, pieces, settle, 0)

    if shared:
        att_copy.wait_send()
        for step in range(2):
            far_weight(step).wait_send()
            pass_weight(step, side).wait_send()

    def drain(d, carry):
        line_sends(d, "wait_send")
        cross_sends(d, "wait_send")
        return carry

    lax.fori_loop(0, lines, drain, 0)


def shared_width(n_head):
    return SHARED_PIECES * PIECE if n_head == 2 else 0


def on_device(n_height, n_head, queries, keys_values, out_weight):
    frames_dev, rows_dev, col_count, width = queries.shape
    model = out_weight.shape[1]
    heads = width // HD
    tokens = frames_dev * rows_dev * col_count
    key_count = rows_dev * VALID_COLS
    share = tokens // n_head
    shared = shared_width(n_head)
    far_width = shared // SHARED_CUTS
    pieces = (model - shared) // PIECE
    assert frames_dev == 2 and rows_dev == PAD_ROWS and col_count == 4 * TILE
    assert n_height % 2 == 0 and n_height * rows_dev <= WINDOW * TILE
    raw = queries.reshape(tokens, width)
    others = n_head - 1
    out = pl.pallas_call(
        functools.partial(kernel, n_height, n_head, rows_dev),
        out_shape=pltpu.VMEM((share // rows_dev, rows_dev, model), jnp.bfloat16),
        in_specs=[
            pl.BlockSpec(memory_space=pltpu.VMEM),
            pl.BlockSpec(memory_space=pl.ANY),
            pl.BlockSpec(memory_space=pl.ANY),
        ],
        out_specs=pl.BlockSpec(memory_space=pltpu.VMEM),
        scratch_shapes=[
            pltpu.VMEM((n_height, 3, 2 * key_count, width), jnp.bfloat16),
            pltpu.VMEM((width, model), jnp.bfloat16),
            pltpu.VMEM((tokens, key_count), jnp.float32),
            pltpu.VMEM((heads, tokens, 1), jnp.float32),
            pltpu.VMEM((heads, tokens, key_count), jnp.float32),
            pltpu.VMEM((heads, tokens, HD), jnp.float32),
            pltpu.VMEM((tokens, width), jnp.bfloat16),
            pltpu.VMEM((others, pieces, share, PIECE), jnp.bfloat16),
            pltpu.VMEM((others, pieces, share, PIECE), jnp.bfloat16),
            pltpu.SemaphoreType.DMA,
            pltpu.SemaphoreType.DMA,
            pltpu.SemaphoreType.DMA((4, n_height, 2 * CUTS)),
            pltpu.SemaphoreType.DMA((n_height, 3 * CUTS)),
            pltpu.SemaphoreType.DMA((others, pieces)),
            pltpu.SemaphoreType.DMA((others, pieces)),
            pltpu.VMEM((SHARED_CUTS, width, max(far_width, HD)), jnp.bfloat16),
            pltpu.VMEM((share, width), jnp.bfloat16),
            pltpu.SemaphoreType.DMA((2,)),
            pltpu.SemaphoreType.DMA((2,)),
            pltpu.SemaphoreType.DMA((SHARED_CUTS,)),
            pltpu.SemaphoreType.DMA((2,)),
            pltpu.VMEM((tokens, width), jnp.bfloat16),
            pltpu.VMEM(keys_values.shape, jnp.bfloat16),
        ],
        compiler_params=pltpu.CompilerParams(
            collective_id=0, has_side_effects=True, vmem_limit_bytes=56 * 2**20
        ),
        name="tile_attention",
    )(raw, keys_values, out_weight)
    return out.reshape(col_count // n_head, frames_dev, rows_dev, model)


def solution(mesh):
    placed = (
        P("tm", "height", None, "head"),
        P(None, "tm", "height", None, "head"),
        P("head", None),
    )
    return jax.shard_map(
        functools.partial(on_device, mesh.shape["height"], mesh.shape["head"]),
        mesh=mesh,
        in_specs=placed,
        out_specs=P("head", "tm", "height", None),
        check_vma=False,
    )
```
